256 devices in a mesh: group: 8 (over x, core), dev: 32 (over y, z).
Axes of the slice: x: 4, y: 4, z: 8, core: 2. Of those that a mesh axis runs over, the one named last changes fastest.
Arguments:
- state: float32 [512, 5, 16, 256], P(('group', 'dev')), as said below
- new_owner: int32 [512], replicated, may hold values from 0 to 255, as said below
- neighbours: int32 [512, 6], replicated, may hold values from -1 to 511, as said below
Outputs:
- new_state: float32 [768, 5, 16, 256], P(('group', 'dev'))
The draws below stay inside these ranges and needn't reach their ends.
Inputs may be any that keep to these rules, and one draw needn't show every extreme that they name: `new_owner`: owners never fall along the box order. Box m's new owner is its old owner m // 2 or the other device of the aligned pair (2 j, 2 j + 1) that holds it, so each device ends with 1 to 3 boxes, and some device holds exactly 3. `neighbours`: boxes sit at distinct points of an integer grid; an entry is -1 where no box is one step away across that face, else that box, always of the same group of 64 consecutive boxes; n is across face 2 a + 1 of m exactly when m is across face 2 a of n. `state`: density and pressure are positive in every cell.
All inputs are finite; a program needn't handle non-finite values.
Results may differ from the reference program's by a relative error of at most 0.0003.
Values sent between devices are 32-bit elements; how exact they have to be, the bound alone decides.
A program may use at most 64 MiB of HBM per device.

```python
import jax
import jax.numpy as jnp
from jax import lax

C = 16
NF = 5
BOX_DEV = 2
BOX_GROUP = 64
NBOX = 512
CAP = 3
N_GROUP = 8
N_DEV = 32


def draw_state(key, part):
    keys = jax.random.split(jax.random.fold_in(key, 3), 3)
    shape = (NBOX, C, C * C)
    rising = 1.0 + 2.0 * jnp.arange(NBOX, dtype=jnp.float32)[:, None, None] / NBOX
    density = jnp.exp(jax.random.uniform(keys[0], shape, jnp.float32, -0.7, 1.4))
    pressure = rising * jnp.exp(jax.random.uniform(keys[1], shape, jnp.float32, -1.6, 0.7))
    speeds = jnp.clip(0.5 * jax.random.normal(keys[2], (3,) + shape, jnp.float32), -2.0, 2.0)
    energy = pressure / 0.4 + 0.5 * density * (speeds[0] * speeds[0] + speeds[1] * speeds[1] + speeds[2] * speeds[2])
    return jnp.stack([density, density * speeds[0], density * speeds[1], density * speeds[2], energy], axis=1)


def draw_new_owner(key, part):
    pair_count = NBOX // (2 * BOX_DEV)
    first_key, second_key = jax.random.split(jax.random.fold_in(key, 5))
    shifts = jax.random.randint(first_key, (pair_count,), -(BOX_DEV - 1), BOX_DEV)
    fullest = jax.random.randint(second_key, (), 0, pair_count)
    shifts = jnp.where(jnp.arange(pair_count) == fullest, BOX_DEV - 1, shifts)
    box_index = jnp.arange(NBOX, dtype=jnp.int32)
    pair_index = box_index // (2 * BOX_DEV)
    within = box_index % (2 * BOX_DEV)
    split_at = BOX_DEV + shifts[pair_index]
    return (2 * pair_index + (within >= split_at).astype(jnp.int32)).astype(jnp.int32)


def morton_part(code, offset):
    total = jnp.zeros_like(code)
    for level in range(7):
        total = total + code // 2 ** (3 * level + offset) % 2 * 2 ** level
    return total


def group_neighbours(key, group):
    candidates = 2 * BOX_GROUP
    code = jnp.arange(candidates, dtype=jnp.int32)
    scores = jax.random.randint(key, (candidates,), 0, 65536) * candidates + code
    picked = jnp.sort(lax.top_k(scores, BOX_GROUP)[1].astype(jnp.int32))
    chosen = jnp.zeros((candidates,), jnp.int32).at[picked].set(1)
    ranking = jnp.cumsum(chosen) - 1
    coords = jnp.stack([morton_part(code, 0), morton_part(code, 1), morton_part(code, 2)], axis=1)
    placed = coords[picked]
    columns = []
    for axis in range(3):
        for side in range(2):
            offset = jnp.zeros((3,), jnp.int32).at[axis].set(2 * side - 1)
            target = placed + offset[None, :]
            match = jnp.all(target[:, None, :] == coords[None, :, :], axis=2) & (chosen[None, :] == 1)
            found = jnp.any(match, axis=1)
            position = jnp.sum(match.astype(jnp.int32) * ranking[None, :], axis=1)
            columns.append(jnp.where(found, group * BOX_GROUP + position, -1))
    return jnp.stack(columns, axis=1).astype(jnp.int32)


def draw_neighbours(key, part):
    group_count = NBOX // BOX_GROUP
    keys = jax.random.split(jax.random.fold_in(key, 7), group_count)
    lists = jax.vmap(group_neighbours)(keys, jnp.arange(group_count, dtype=jnp.int32))
    return lists.reshape(NBOX, 6).astype(jnp.int32)


def setup_inputs(seed: int = 0) -> dict:
    key_list = jax.random.split(jax.random.key(seed), 4)
    state = draw_state(jax.random.fold_in(key_list[3], 71), 0)
    new_owner = draw_new_owner(jax.random.fold_in(key_list[3], 71), 0)
    neighbours = draw_neighbours(jax.random.fold_in(key_list[3], 71), 0)
    return {"state": state, "new_owner": new_owner, "neighbours": neighbours}


GAMMA = 1.4
COURANT = 0.3

def primitive(conserved):
    density = conserved[0]
    vel_x = conserved[1] / density
    vel_y = conserved[2] / density
    vel_z = conserved[3] / density
    pressure = (GAMMA - 1.0) * (conserved[4] - 0.5 * density * (vel_x * vel_x + vel_y * vel_y + vel_z * vel_z))
    return (density, vel_x, vel_y, vel_z, pressure)

def minmod(lower, upper):
    return 0.5 * (jnp.sign(lower) + jnp.sign(upper)) * jnp.minimum(jnp.abs(lower), jnp.abs(upper))

def flux_parts(states, normal):
    density, vel_x, vel_y, vel_z, pressure = states
    normal_speed = (vel_x, vel_y, vel_z)[normal]
    energy = pressure / (GAMMA - 1.0) + 0.5 * density * (vel_x * vel_x + vel_y * vel_y + vel_z * vel_z)
    conserved = (density, density * vel_x, density * vel_y, density * vel_z, energy)
    fluxes = [item * normal_speed for item in conserved]
    fluxes[1 + normal] = fluxes[1 + normal] + pressure
    fluxes[4] = fluxes[4] + pressure * normal_speed
    sound = jnp.sqrt(GAMMA * pressure / density)
    return (conserved, fluxes, normal_speed, sound)

def hll(left, right, normal):
    cons_left, flux_left, speed_left, sound_left = flux_parts(left, normal)
    cons_right, flux_right, speed_right, sound_right = flux_parts(right, normal)
    slowest = jnp.minimum(jnp.minimum(speed_left - sound_left, speed_right - sound_right), 0.0)
    fastest = jnp.maximum(jnp.maximum(speed_left + sound_left, speed_right + sound_right), 0.0)
    spread = fastest - slowest
    return tuple(((fastest * flux_a - slowest * flux_b + slowest * fastest * (cons_b - cons_a)) / spread for flux_a, flux_b, cons_a, cons_b in zip(flux_left, flux_right, cons_left, cons_right)))

def along(field, begin, finish, axis):
    return lax.slice_in_dim(field, begin, finish, axis=axis)

def difference(states, normal):
    inner = []
    for field in states:
        for other in range(3):
            if other != normal:
                field = along(field, 2, 2 + C, other)
        inner.append(field)
    slopes = []
    for field in inner:
        jumps = along(field, 1, C + 4, normal) - along(field, 0, C + 3, normal)
        slopes.append(minmod(along(jumps, 0, C + 2, normal), along(jumps, 1, C + 3, normal)))
    left = tuple((along(field, 1, C + 2, normal) + 0.5 * along(slope, 0, C + 1, normal) for field, slope in zip(inner, slopes)))
    right = tuple((along(field, 2, C + 3, normal) - 0.5 * along(slope, 1, C + 2, normal) for field, slope in zip(inner, slopes)))
    fluxes = hll(left, right, normal)
    return tuple((along(flux, 1, C + 1, normal) - along(flux, 0, C, normal) for flux in fluxes))

def advance(padded, ratio):
    states = primitive(padded)
    parts = [difference(states, normal) for normal in range(3)]
    inside = padded[:, 2:2 + C, 2:2 + C, 2:2 + C]
    total = jnp.stack([parts[0][index] + parts[1][index] + parts[2][index] for index in range(NF)])
    return inside - ratio * total

def padded_box(boxes, neighbours, index):
    inside = boxes[index]
    padded = jnp.pad(inside, ((0, 0), (2, 2), (2, 2), (2, 2)), mode='edge')
    for axis in range(3):
        for side in range(2):
            other = neighbours[index, 2 * axis + side]
            source = boxes[jnp.maximum(other, 0)]
            if side == 0:
                layers = lax.slice_in_dim(source, C - 2, C, axis=1 + axis)
            else:
                layers = lax.slice_in_dim(source, 0, 2, axis=1 + axis)
            spots = [slice(None), slice(2, 2 + C), slice(2, 2 + C), slice(2, 2 + C)]
            spots[1 + axis] = slice(0, 2) if side == 0 else slice(C + 2, C + 4)
            spots = tuple(spots)
            padded = padded.at[spots].set(jnp.where(other >= 0, layers, padded[spots]))
    return padded

def fastest_signal(box):
    density, vel_x, vel_y, vel_z, pressure = primitive(box)
    quickest = jnp.maximum(jnp.maximum(jnp.abs(vel_x), jnp.abs(vel_y)), jnp.abs(vel_z))
    return jnp.max(quickest + jnp.sqrt(GAMMA * pressure / density))

def reference(state, new_owner, neighbours):
    boxes = state.reshape(NBOX, NF, C, C, C)
    highest = jnp.max(lax.map(fastest_signal, boxes))
    ratio = COURANT / highest
    updated = lax.map(lambda index: advance(padded_box(boxes, neighbours, index), ratio), jnp.arange(NBOX, dtype=jnp.int32))
    device_count = N_GROUP * N_DEV
    owners = jnp.arange(device_count, dtype=jnp.int32)
    counts = lax.optimization_barrier(jnp.sum((new_owner[None, :] == owners[:, None]).astype(jnp.int32), axis=1))
    firsts = lax.optimization_barrier(jnp.sum((new_owner[None, :] < owners[:, None]).astype(jnp.int32), axis=1))
    slot_index = jnp.arange(CAP, dtype=jnp.int32)
    source = (firsts[:, None] + slot_index[None, :]).reshape(-1)
    usable = (slot_index[None, :] < counts[:, None]).reshape(-1)
    picked = updated[jnp.minimum(source, NBOX - 1)]
    result = jnp.where(usable[:, None, None, None, None], picked, jnp.zeros_like(picked))
    return result.reshape(device_count * CAP, NF, C, C * C)
```

```python
import functools

import jax
import jax.numpy as jnp
from jax import lax
from jax.experimental import pallas as pl
from jax.experimental.pallas import tpu as pltpu
from jax.sharding import PartitionSpec as P

GAMMA = 1.4
COURANT = 0.3
MESH = pl.DeviceIdType.MESH
EDGE = 16
PLANE = 256
FIELDS = 5
FACES = 12
UNIT = 40
GROUPS = 8
DEVS = 32
ROWS_Y = 4
COLS_Z = 8


def primitive(conserved):
    density = conserved[0]
    vel_x = conserved[1] / density
    vel_y = conserved[2] / density
    vel_z = conserved[3] / density
    pressure = (GAMMA - 1.0) * (
        conserved[4] - 0.5 * density * (vel_x * vel_x + vel_y * vel_y + vel_z * vel_z)
    )
    return (density, vel_x, vel_y, vel_z, pressure)


def minmod(lower, upper):
    return jnp.maximum(jnp.minimum(lower, upper), 0.0) + jnp.minimum(jnp.maximum(lower, upper), 0.0)


def flux_parts(states, normal):
    density, vel_x, vel_y, vel_z, pressure = states
    normal_speed = (vel_x, vel_y, vel_z)[normal]
    energy = pressure * (1.0 / (GAMMA - 1.0)) + 0.5 * density * (
        vel_x * vel_x + vel_y * vel_y + vel_z * vel_z
    )
    conserved = (density, density * vel_x, density * vel_y, density * vel_z, energy)
    fluxes = [item * normal_speed for item in conserved]
    fluxes[1 + normal] = fluxes[1 + normal] + pressure
    fluxes[4] = fluxes[4] + pressure * normal_speed
    sound = jnp.sqrt(GAMMA * pressure / density)
    return (conserved, fluxes, normal_speed, sound)


def hll(left, right, normal):
    cons_left, flux_left, speed_left, sound_left = flux_parts(left, normal)
    cons_right, flux_right, speed_right, sound_right = flux_parts(right, normal)
    slowest = jnp.minimum(jnp.minimum(speed_left - sound_left, speed_right - sound_right), 0.0)
    fastest = jnp.maximum(jnp.maximum(speed_left + sound_left, speed_right + sound_right), 0.0)
    scale = 1.0 / (fastest - slowest)
    product = slowest * fastest
    return [
        (fastest * flux_a - slowest * flux_b + product * (cons_b - cons_a)) * scale
        for flux_a, flux_b, cons_a, cons_b in zip(flux_left, flux_right, cons_left, cons_right)
    ]


def swap_matrix(columns, pick):
    source = lax.broadcasted_iota(jnp.int32, (PLANE, columns), 0)
    lane = lax.broadcasted_iota(jnp.int32, (PLANE, columns), 1)
    wanted = (lane % EDGE) * EDGE + pick(lane // EDGE)
    return (source == wanted).astype(jnp.float32).astype(jnp.bfloat16)


def exact_permute(values, matrix):
    high = values.astype(jnp.bfloat16)
    rest = values - high.astype(jnp.float32)
    middle = rest.astype(jnp.bfloat16)
    low = (rest - middle.astype(jnp.float32)).astype(jnp.bfloat16)
    dot = functools.partial(jnp.dot, preferred_element_type=jnp.float32)
    return dot(high, matrix) + (dot(middle, matrix) + dot(low, matrix))


def lanes(rows):
    return lax.broadcasted_iota(jnp.int32, (rows, 128), 1)


def by_group(pieces, rows, begin):
    group = lanes(rows) // 32
    out = None
    for index, piece in enumerate(pieces):
        shift = (32 * index - begin) % 128
        moved = piece if shift == 0 else pltpu.roll(piece, shift, 1)
        out = moved if out is None else jnp.where(group == index, moved, out)
    return out


def pack_faces(x_ref, main_ref, extra_ref):
    half = lanes(8) < 64
    upper = lax.broadcasted_iota(jnp.int32, (8, 128), 0) < 4
    matrix = swap_matrix(128, lambda layer: jnp.where(layer < 2, layer, layer + 8))
    for box in range(2):
        cells = [x_ref[box, field] for field in range(FIELDS)]
        turned = exact_permute(jnp.concatenate(cells, axis=0), matrix)
        for side in range(2):
            first = 0 if side == 0 else EDGE - 2
            face = box * 6 + side
            for field in range(4):
                for layer in range(2):
                    for part in range(2):
                        row = 4 * field + 2 * layer + part
                        main_ref[face, row : row + 1, :] = x_ref[
                            box, field, first + layer : first + layer + 1, 128 * part : 128 * part + 128
                        ]
            for copy in range(2):
                for layer in range(2):
                    for part in range(2):
                        row = 4 * copy + 2 * layer + part
                        extra_ref[face, row : row + 1, :] = x_ref[
                            box, 4, first + layer : first + layer + 1, 128 * part : 128 * part + 128
                        ]
            twice = extra_ref[face]
            extra_ref[face] = jnp.where(half == upper, twice, pltpu.roll(twice, 64, 1))
            begin = 96 * side
            for axis in (1, 2):
                if axis == 1:
                    tiles = [cell[:, 128 * side : 128 * side + 128] for cell in cells]
                else:
                    tiles = [turned[EDGE * f : EDGE * f + EDGE] for f in range(FIELDS)]
                face = box * 6 + 2 * axis + side
                main_ref[face] = by_group(tiles[:4], EDGE, begin)
                last = tiles[4]
                extra_ref[face] = by_group([last[0:8], last[8:16]] * 2, 8, begin)
    main_ref[FACES] = jnp.zeros((EDGE, 128), jnp.float32)
    extra_ref[FACES] = jnp.zeros((8, 128), jnp.float32)


def local_signal(x_ref):
    best = None
    for box in range(2):
        density, vel_x, vel_y, vel_z, pressure = primitive([x_ref[box, f] for f in range(FIELDS)])
        quickest = jnp.maximum(jnp.maximum(jnp.abs(vel_x), jnp.abs(vel_y)), jnp.abs(vel_z))
        signal = quickest + jnp.sqrt(GAMMA * pressure / density)
        for row in range(2):
            for column in range(2):
                tile = signal[8 * row : 8 * row + 8, 128 * column : 128 * column + 128]
                best = tile if best is None else jnp.maximum(best, tile)
    return best


def share_kernel(base, table_ref, x_ref, got_ref, top_ref, main, extra, out, tops, ssem, rsem, tsem, usem):
    group = lax.axis_index("group")
    dev = lax.axis_index("dev")
    row, column = dev // COLS_Z, dev % COLS_Z
    barrier = pltpu.get_barrier_semaphore()

    def along_dev(step):
        return (group, lax.rem(dev + step, DEVS))

    stages = (
        (GROUPS, lambda step: (lax.rem(group + step, GROUPS), dev)),
        (ROWS_Y, lambda step: (group, lax.rem(row + step, ROWS_Y) * COLS_Z + column)),
        (COLS_Z, lambda step: (group, row * COLS_Z + lax.rem(column + step, COLS_Z))),
    )

    def greet(step, carry):
        pl.semaphore_signal(barrier, inc=1, device_id=along_dev(step), device_id_type=MESH)
        return carry

    lax.fori_loop(1, DEVS, greet, 0)
    if base == 0:
        for step in range(1, GROUPS):
            pl.semaphore_signal(barrier, inc=1, device_id=stages[0][1](step), device_id_type=MESH)
        tops[0, 0] = local_signal(x_ref)
    pack_faces(x_ref, main, extra)
    pl.semaphore_wait(barrier, DEVS - 1 + (GROUPS - 1 if base == 0 else 0))

    def small(stage, step):
        return pltpu.make_async_remote_copy(
            tops.at[stage, 0],
            tops.at[stage, step],
            tsem.at[stage, step],
            usem.at[stage, step],
            device_id=stages[stage][1](step),
            device_id_type=MESH,
        )

    def send_top(stage):
        for step in range(1, stages[stage][0]):
            small(stage, step).start()

    def take_top(stage):
        count = stages[stage][0]
        for step in range(1, count):
            small(stage, step).wait()
        best = tops[stage, 0]
        for step in range(1, count):
            best = jnp.maximum(best, tops[stage, step])
        return best

    def large(step):
        return pltpu.make_async_remote_copy(
            out.at[step],
            got_ref.at[step],
            ssem.at[step],
            rsem.at[step],
            device_id=along_dev(step),
            device_id_type=MESH,
        )

    half = lanes(8) < 64

    def fill(step, where):
        one = table_ref[4 * step + base]
        two = table_ref[4 * step + base + 1]
        where[step, 0:16, :] = main[one]
        where[step, 16:32, :] = main[two]
        where[step, 32:40, :] = jnp.where(half, extra[one], extra[two])

    def send(step, carry):
        fill(step, out)
        large(step).start()
        return carry

    if base == 0:
        send_top(0)
        lax.fori_loop(1, DEVS // 2, send, 0)
        tops[1, 0] = take_top(0)
        send_top(1)
        lax.fori_loop(DEVS // 2, DEVS, send, 0)
        fill(0, got_ref)
        tops[2, 0] = take_top(1)
        send_top(2)
        top_ref[...] = take_top(2)
    else:
        lax.fori_loop(1, DEVS, send, 0)
        fill(0, got_ref)
        top_ref[...] = jnp.zeros((8, 128), jnp.float32)

    def finish(step, carry):
        large(step).wait()
        return carry

    lax.fori_loop(1, DEVS, finish, 0)


def share(table, state, base):
    vmem = pl.BlockSpec(memory_space=pltpu.VMEM)
    return pl.pallas_call(
        functools.partial(share_kernel, base),
        out_shape=(
            jax.ShapeDtypeStruct((DEVS, UNIT, 128), jnp.float32),
            jax.ShapeDtypeStruct((8, 128), jnp.float32),
        ),
        in_specs=[pl.BlockSpec(memory_space=pltpu.SMEM), vmem],
        out_specs=(vmem, vmem),
        scratch_shapes=[
            pltpu.VMEM((FACES + 1, EDGE, 128), jnp.float32),
            pltpu.VMEM((FACES + 1, 8, 128), jnp.float32),
            pltpu.VMEM((DEVS, UNIT, 128), jnp.float32),
            pltpu.VMEM((3, 8, 8, 128), jnp.float32),
            pltpu.SemaphoreType.DMA((DEVS,)),
            pltpu.SemaphoreType.DMA((DEVS,)),
            pltpu.SemaphoreType.DMA((3, 8)),
            pltpu.SemaphoreType.DMA((3, 8)),
        ],
        compiler_params=pltpu.CompilerParams(
            collective_id=base, has_side_effects=True, vmem_limit_bytes=32 << 20
        ),
    )(table, state)


def rolled(arrays, amount, axis):
    return [pltpu.roll(a, amount % a.shape[axis], axis) for a in arrays]


def difference(states, normal, axis, unit):
    lefts, rights = [], []
    for field in states:
        (before,) = rolled([field], unit, axis)
        jump = field - before
        (after,) = rolled([jump], -unit, axis)
        half = 0.5 * minmod(jump, after)
        lefts.append(field + half)
        rights.append(field - half)
    fluxes = hll(rolled(lefts, unit, axis), rights, normal)
    return [high - low for high, low in zip(rolled(fluxes, -unit, axis), fluxes)]


def face_tile(ghosts, absent, present_low, present_high):
    lane = lanes(EDGE)
    low = jnp.where(present_low, ghosts[0], absent[0])
    high = jnp.where(present_high, ghosts[1], absent[1])
    return jnp.where(lane < 64, high, low)


def step_kernel(slots, where_ref, x_ref, got_ref, top_ref, out_ref, turned_ref, total_ref):
    ratio = COURANT / jnp.max(top_ref[...], axis=(0, 1), keepdims=True)
    matrix = swap_matrix(PLANE, lambda layer: layer)
    lane = lanes(EDGE)
    half = lanes(8) < 64
    row8 = lax.broadcasted_iota(jnp.int32, (8, PLANE), 0)

    def fetch(box, face):
        step = where_ref[box * 6 + face]
        slot = where_ref[FACES + box * 6 + face]
        present = where_ref[2 * FACES + box * 6 + face]
        begin = (slot // 2) * UNIT
        main = got_ref[step, pl.ds(pl.multiple_of(begin + (slot % 2) * 16, 8), 16), :]
        extra = got_ref[step, pl.ds(pl.multiple_of(begin + 32, 8), 8), :]
        extra = jnp.where(slot % 2 == 0, extra, pltpu.roll(extra, 64, 1))
        return main, extra, present > 0

    def lane_ghosts(main, extra, target):
        out = []
        for field in range(4):
            out.append(pltpu.roll(main, (target - 32 * field) % 128, 1))
        first = pltpu.roll(extra, target % 128, 1)
        second = pltpu.roll(extra, (target - 32) % 128, 1)
        out.append(jnp.concatenate([first, second], axis=0))
        return out

    def row_ghosts(main, extra):
        out = []
        last = jnp.where(half[0:4], extra[0:4], pltpu.roll(extra, 64, 1)[4:8])
        for field in range(FIELDS):
            rows = main[4 * field : 4 * field + 4] if field < 4 else last
            out.append(
                [
                    jnp.concatenate([rows[2 * layer : 2 * layer + 1], rows[2 * layer + 1 : 2 * layer + 2]], axis=1)
                    for layer in range(2)
                ]
            )
        return out

    def one_box(box, carry):
        cells = [x_ref[box, field] for field in range(FIELDS)]
        turned_ref[...] = exact_permute(jnp.concatenate(cells, axis=0), matrix)
        low_main, low_extra, low_there = fetch(box, 0)
        high_main, high_extra, high_there = fetch(box, 1)
        low = row_ghosts(low_main, low_extra)
        high = row_ghosts(high_main, high_extra)
        extended = []
        for field in range(FIELDS):
            edge_low = cells[field][0:1]
            edge_high = cells[field][EDGE - 1 : EDGE]
            l0 = jnp.where(low_there, low[field][0], edge_low)
            l1 = jnp.where(low_there, low[field][1], edge_low)
            h0 = jnp.where(high_there, high[field][0], edge_high)
            h1 = jnp.where(high_there, high[field][1], edge_high)
            tile = jnp.where(row8 == 0, h0, jnp.where(row8 == 7, l1, jnp.where(row8 == 6, l0, h1)))
            extended.append(jnp.concatenate([cells[field], tile], axis=0))
        for part in range(2):
            states = primitive([e[:, 128 * part : 128 * part + 128] for e in extended])
            parts = difference(states, 0, 0, 1)
            for field in range(FIELDS):
                total_ref[field, :, 128 * part : 128 * part + 128] = parts[field][0:EDGE]
        for axis in (2, 1):
            if axis == 1:
                source = cells
            else:
                source = [turned_ref[EDGE * f : EDGE * f + EDGE] for f in range(FIELDS)]
            low_main, low_extra, low_there = fetch(box, 2 * axis)
            high_main, high_extra, high_there = fetch(box, 2 * axis + 1)
            low = lane_ghosts(low_main, low_extra, 96)
            high = lane_ghosts(high_main, high_extra, 0)
            extended = []
            for field in range(FIELDS):
                left, right = source[field][:, 0:128], source[field][:, 128:256]
                edge_low = jnp.where(lane < 112, pltpu.roll(left, 96, 1), pltpu.roll(left, 112, 1))
                edge_high = jnp.where(lane < 16, pltpu.roll(right, 16, 1), pltpu.roll(right, 32, 1))
                tile = face_tile((low[field], high[field]), (edge_low, edge_high), low_there, high_there)
                extended.append(jnp.concatenate([left, right, tile], axis=1))
            pieces = []
            for part in range(2):
                states = primitive([e[8 * part : 8 * part + 8] for e in extended])
                pieces.append(difference(states, axis, 1, EDGE))
            if axis == 2:
                stacked = jnp.concatenate(
                    [pieces[part][f][:, 0:PLANE] for f in range(FIELDS) for part in range(2)], axis=0
                )
                turned_ref[...] = exact_permute(stacked, matrix)
            else:
                for field in range(FIELDS):
                    along = jnp.concatenate([pieces[part][field][:, 0:PLANE] for part in range(2)], axis=0)
                    total = (total_ref[field] + along) + turned_ref[EDGE * field : EDGE * field + EDGE]
                    out_ref[box, field] = cells[field] - ratio * total
        return carry

    lax.fori_loop(0, 2, one_box, 0)


def advance(where, state, got, top, slots):
    vmem = pl.BlockSpec(memory_space=pltpu.VMEM)
    return pl.pallas_call(
        functools.partial(step_kernel, slots),
        out_shape=jax.ShapeDtypeStruct(state.shape, state.dtype),
        in_specs=[pl.BlockSpec(memory_space=pltpu.SMEM), vmem, vmem, vmem],
        out_specs=vmem,
        scratch_shapes=[
            pltpu.VMEM((FIELDS * EDGE, PLANE), jnp.float32),
            pltpu.VMEM((FIELDS, EDGE, PLANE), jnp.float32),
        ],
        compiler_params=pltpu.CompilerParams(vmem_limit_bytes=32 << 20),
    )(where, state, got, top)


def tables(near, dev):
    face = jnp.arange(FACES, dtype=jnp.int32)
    there = near >= 0
    other = jnp.where(there, (near // 2) % DEVS, -1)
    same = (other[:, None] == other[None, :]) & there[:, None] & there[None, :]
    rank = jnp.sum((same & (face[None, :] < face[:, None])).astype(jnp.int32), axis=1)
    far_face = (near % 2) * 6 + ((face % 6) ^ 1)
    far_rank = jnp.sum((same & (far_face[None, :] < far_face[:, None])).astype(jnp.int32), axis=1)
    place = jnp.where(there, ((other - dev + DEVS) % DEVS) * 4 + rank, -1)
    spot = jnp.arange(4 * DEVS, dtype=jnp.int32)
    hit = spot[:, None] == place[None, :]
    table = FACES + jnp.sum(jnp.where(hit, face[None, :] - FACES, 0), axis=1)
    step = jnp.where(there, (dev - other + DEVS) % DEVS, 0)
    where = jnp.concatenate([step, jnp.where(there, far_rank, 0), there.astype(jnp.int32)])
    return table, where


def most_shared(neighbours):
    near = neighbours.reshape(-1, FACES)
    owner = jnp.where(near >= 0, near // 2, -1)
    same = (owner[:, :, None] == owner[:, None, :]) & (owner >= 0)[:, :, None]
    return jnp.max(jnp.sum(same.astype(jnp.int32), axis=2))


def body(state, new_owner, neighbours):
    group = lax.axis_index("group")
    dev = lax.axis_index("dev")
    place = group * DEVS + dev
    near = lax.dynamic_slice_in_dim(neighbours, 2 * place, 2, 0).reshape(FACES)
    table, where = tables(near, dev)
    got, top = share(table, state, 0)

    def few(state):
        return advance(where, state, got, top, 2)

    def many(state):
        more, _ = share(table, state, 2)
        return advance(where, state, jnp.concatenate([got, more], axis=1), top, 4)

    fresh = lax.cond(most_shared(neighbours) > 2, many, few, state)
    parity = dev % 2
    route = [(d, d ^ 1) for d in range(DEVS)]
    sent = lax.ppermute(jnp.where(parity == 0, fresh[1], fresh[0]), "dev", route)
    first = place // 2 * 4
    owners = lax.dynamic_slice_in_dim(new_owner, first, 4, 0)
    split = jnp.sum((owners == place // 2 * 2).astype(jnp.int32))
    none = jnp.zeros_like(sent)
    pick = lambda test, a, b: jnp.where(test, a, b)
    even = (fresh[0], pick(split >= 2, fresh[1], none), pick(split == 3, sent, none))
    odd = (
        pick(split == 1, sent, pick(split == 2, fresh[0], fresh[1])),
        pick(split == 1, fresh[0], pick(split == 2, fresh[1], none)),
        pick(split == 1, fresh[1], none),
    )
    return jnp.stack([pick(parity == 0, a, b) for a, b in zip(even, odd)])


def solution(mesh):
    placed = (P(("group", "dev"), None, None, None), P(), P())
    return jax.shard_map(
        body,
        mesh=mesh,
        in_specs=placed,
        out_specs=P(("group", "dev"), None, None, None),
        check_vma=False,
    )
```

```python
import functools

import jax
import jax.numpy as jnp
from jax import lax
from jax.experimental import pallas as pl
from jax.experimental.pallas import tpu as pltpu
from jax.sharding import PartitionSpec as P

GAMMA = 1.4
COURANT = 0.3
MESH = pl.DeviceIdType.MESH
EDGE = 16
PLANE = 256
FIELDS = 5
FACES = 12
UNIT = 5
RECORD = 3
OWN = (FACES + 1) * RECORD
CAP_Z = 5
CAP_Y = 6
CAP_HERE = 12


def unit_tiles(cap):
    return 2 * cap + (cap + 1) // 2


UNIT_Z = unit_tiles(CAP_Z)
UNIT_Y = unit_tiles(CAP_Y)
HERE = 3 * UNIT_Y
GROUPS = 8
DEVS = 32
ROWS_Y = 4
COLS_Z = 8


def primitive(conserved):
    density = conserved[0]
    vel_x = conserved[1] / density
    vel_y = conserved[2] / density
    vel_z = conserved[3] / density
    pressure = (GAMMA - 1.0) * (
        conserved[4] - 0.5 * density * (vel_x * vel_x + vel_y * vel_y + vel_z * vel_z)
    )
    return (density, vel_x, vel_y, vel_z, pressure)


def minmod(lower, upper):
    return jnp.maximum(jnp.minimum(lower, upper), 0.0) + jnp.minimum(jnp.maximum(lower, upper), 0.0)


def flux_parts(states, normal):
    density, vel_x, vel_y, vel_z, pressure = states
    normal_speed = (vel_x, vel_y, vel_z)[normal]
    energy = pressure * (1.0 / (GAMMA - 1.0)) + 0.5 * density * (
        vel_x * vel_x + vel_y * vel_y + vel_z * vel_z
    )
    conserved = (density, density * vel_x, density * vel_y, density * vel_z, energy)
    fluxes = [item * normal_speed for item in conserved]
    fluxes[1 + normal] = fluxes[1 + normal] + pressure
    fluxes[4] = fluxes[4] + pressure * normal_speed
    sound = jnp.sqrt(GAMMA * pressure / density)
    return (conserved, fluxes, normal_speed, sound)


def hll(left, right, normal):
    cons_left, flux_left, speed_left, sound_left = flux_parts(left, normal)
    cons_right, flux_right, speed_right, sound_right = flux_parts(right, normal)
    slowest = jnp.minimum(jnp.minimum(speed_left - sound_left, speed_right - sound_right), 0.0)
    fastest = jnp.maximum(jnp.maximum(speed_left + sound_left, speed_right + sound_right), 0.0)
    scale = 1.0 / (fastest - slowest)
    product = slowest * fastest
    return [
        (fastest * flux_a - slowest * flux_b + product * (cons_b - cons_a)) * scale
        for flux_a, flux_b, cons_a, cons_b in zip(flux_left, flux_right, cons_left, cons_right)
    ]


def swap_matrix(columns, pick):
    source = lax.broadcasted_iota(jnp.int32, (PLANE, columns), 0)
    lane = lax.broadcasted_iota(jnp.int32, (PLANE, columns), 1)
    wanted = (lane % EDGE) * EDGE + pick(lane // EDGE)
    return (source == wanted).astype(jnp.float32).astype(jnp.bfloat16)


def exact_permute(values, matrix):
    high = values.astype(jnp.bfloat16)
    rest = values - high.astype(jnp.float32)
    middle = rest.astype(jnp.bfloat16)
    low = (rest - middle.astype(jnp.float32)).astype(jnp.bfloat16)
    dot = functools.partial(jnp.dot, preferred_element_type=jnp.float32)
    return dot(high, matrix) + (dot(middle, matrix) + dot(low, matrix))


def lanes(rows):
    return lax.broadcasted_iota(jnp.int32, (rows, 128), 1)


def by_group(pieces, rows, begin):
    group = lanes(rows) // 32
    out = None
    for index, piece in enumerate(pieces):
        shift = (32 * index - begin) % 128
        moved = piece if shift == 0 else pltpu.roll(piece, shift, 1)
        out = moved if out is None else jnp.where(group == index, moved, out)
    return out


def pack_faces(x_ref, pool):
    half = lanes(8) < 64
    upper = lax.broadcasted_iota(jnp.int32, (8, 128), 0) < 4
    matrix = swap_matrix(128, lambda layer: jnp.where(layer < 2, layer, layer + 8))
    for box in range(2):
        cells = [x_ref[box, field] for field in range(FIELDS)]
        turned = exact_permute(jnp.concatenate(cells, axis=0), matrix)
        for side in range(2):
            first = 0 if side == 0 else EDGE - 2
            begin = RECORD * (box * 6 + side)
            for place in range(24):
                field, layer, part = min(place // 4, 4), place // 2 % 2, place % 2
                pool[begin + place // 8, place % 8 : place % 8 + 1, :] = x_ref[
                    box, field, first + layer : first + layer + 1, 128 * part : 128 * part + 128
                ]
            twice = pool[begin + 2]
            pool[begin + 2] = jnp.where(half == upper, twice, pltpu.roll(twice, 64, 1))
            source = 96 * side
            for axis in (1, 2):
                if axis == 1:
                    tiles = [cell[:, 128 * side : 128 * side + 128] for cell in cells]
                else:
                    tiles = [turned[EDGE * f : EDGE * f + EDGE] for f in range(FIELDS)]
                begin = RECORD * (box * 6 + 2 * axis + side)
                main = by_group(tiles[:4], EDGE, source)
                pool[begin] = main[0:8]
                pool[begin + 1] = main[8:16]
                last = tiles[4]
                pool[begin + 2] = by_group([last[0:8], last[8:16]] * 2, 8, source)
    for tile in range(RECORD * FACES, OWN):
        pool[tile] = jnp.zeros((8, 128), jnp.float32)


def local_signal(x_ref):
    best = None
    for box in range(2):
        density, vel_x, vel_y, vel_z, pressure = primitive([x_ref[box, f] for f in range(FIELDS)])
        quickest = jnp.maximum(jnp.maximum(jnp.abs(vel_x), jnp.abs(vel_y)), jnp.abs(vel_z))
        signal = quickest + jnp.sqrt(GAMMA * pressure / density)
        for row in range(2):
            for column in range(2):
                tile = signal[8 * row : 8 * row + 8, 128 * column : 128 * column + 128]
                best = tile if best is None else jnp.maximum(best, tile)
    return best


def fill_tables(near_ref, row, column, tab):
    square = (128, 128)
    index = lax.broadcasted_iota(jnp.int32, square, 0)
    lane = lax.broadcasted_iota(jnp.int32, square, 1)
    spread = (
        lax.broadcasted_iota(jnp.int32, (6, 128), 1) % 8 == lax.broadcasted_iota(jnp.int32, (6, 128), 0)
    ).astype(jnp.float32)
    tiled = jnp.dot(
        near_ref[...].astype(jnp.float32), spread, precision=lax.Precision.HIGHEST, preferred_element_type=jnp.float32
    )
    here = lanes(16) // 8 == lax.broadcasted_iota(jnp.int32, (16, 128), 0)
    flat = jnp.sum(jnp.where(here, tiled, 0.0), axis=0, keepdims=True)
    across = jnp.broadcast_to(flat, square)
    down = jnp.transpose(across)

    def facts(values, q):
        near = values.astype(jnp.int32)
        there = (near >= 0) & (q % 8 < 6)
        other = (near // 2) % DEVS
        far_row, far_column = other // COLS_Z, other % COLS_Z
        far_face = (near % 2) * 6 + (q % 8) + 1 - 2 * (q % 2)
        return there, far_row, far_column, far_face

    there, far_row, far_column, far_face = facts(down, index)
    there_j, far_row_j, far_column_j, far_face_j = facts(across, lane)
    ones = jnp.ones(square, jnp.bfloat16)

    def rank(test):
        hits = jnp.where(test, 1.0, 0.0).astype(jnp.bfloat16)
        return jnp.dot(hits, ones, preferred_element_type=jnp.float32).astype(jnp.int32)

    source = index // 16
    own = there & (source == column)
    before = (source == lane // 16) & (lane < index) & there_j
    rank_z = rank(before & (far_column_j == far_column))
    rank_here = rank(before & (far_row_j == far_row))
    held = there & (far_column == column)
    held_j = there_j & (far_column_j == column)
    rank_y = rank(held_j & (far_row_j == far_row) & (far_face_j < far_face))

    def total(test, values):
        return jnp.sum(jnp.where(test, values, 0), axis=0, keepdims=True)

    face = (index // 8 % 2) * 6 + index % 8
    step = (far_column - column + COLS_Z) % COLS_Z
    fits = own & (step > 0) & (rank_z < CAP_Z)
    hit = fits & (step * CAP_Z + rank_z == lane)
    tab[0:1, :] = RECORD * FACES + total(hit, RECORD * (face - FACES))
    over = own & (step > 0) & (rank_z >= CAP_Z)
    back = (column - source + COLS_Z) % COLS_Z
    begin = OWN + (back - 1) * UNIT_Z
    main = jnp.where(back == 0, RECORD * face, begin + 2 * rank_z)
    last = jnp.where(back == 0, RECORD * face + 2, begin + 2 * CAP_Z + rank_z // 2)
    side = jnp.where(back == 0, 0, rank_z % 2)
    step = (far_row - row + ROWS_Y) % ROWS_Y
    near_by = step == 0
    base = jnp.where(near_by, 3 * CAP_Y, (step - 1) * CAP_Y)
    fits = held & (near_by | (rank_y < CAP_Y))
    hit = fits & (base + rank_y == lane)
    tab[1:2, :] = RECORD * FACES + total(hit, main - RECORD * FACES)
    tab[2:3, :] = RECORD * FACES + 2 + total(hit, last - RECORD * FACES - 2)
    tab[3:4, :] = total(hit, side)
    step = (row - far_row + ROWS_Y) % ROWS_Y
    near_by = step == 0
    over = over | (own & ~near_by & (rank_here >= CAP_Y))
    begin = jnp.where(near_by, HERE, (step - 1) * UNIT_Y)
    cap = jnp.where(near_by, CAP_HERE, CAP_Y)
    hit = own & (near_by | (rank_here < CAP_Y)) & (face == lane)
    tab[4:5, :] = total(hit, begin + 2 * rank_here)
    tab[5:6, :] = total(hit, begin + 2 * cap + rank_here // 2)
    tab[6:7, :] = total(hit, rank_here % 2)
    tab[7:8, :] = total(hit, 1)
    return jnp.max(jnp.where(over, 1.0, 0.0), axis=0, keepdims=True)


def move_records(pool, entries, target, start):
    half = lanes(8) < 64
    cap = len(entries)
    for index, (main, _, _) in enumerate(entries):
        target[start + 2 * index] = pool[main]
        target[start + 2 * index + 1] = pool[main + 1]

    def last(entry, wanted):
        tile = pool[entry[1]]
        if entry[2] is None:
            return tile
        side = jnp.full((8, 128), entry[2], jnp.int32)
        return jnp.where(side == wanted, tile, pltpu.roll(tile, 64, 1))

    for pair in range((cap + 1) // 2):
        tile = last(entries[2 * pair], 0)
        if 2 * pair + 1 < cap:
            tile = jnp.where(half, tile, last(entries[2 * pair + 1], 1))
        target[start + 2 * cap + pair] = tile


def share_kernel(
    x_hbm, near_hbm, got_ref, top_ref, tab_ref, x_ref, near_ref, tab, own, pool, out_z, out_y, tops,
    insem, zsend, zgot, ysend, ygot, tsend, tgot,
):
    group = lax.axis_index("group")
    dev = lax.axis_index("dev")
    row, column = dev // COLS_Z, dev % COLS_Z
    start = pl.multiple_of((group * ROWS_Y + row) * 2 * COLS_Z, 16)
    load_near = pltpu.make_async_copy(near_hbm.at[pl.ds(start, 2 * COLS_Z), :], near_ref, insem.at[0])
    load_x = pltpu.make_async_copy(x_hbm, x_ref, insem.at[1])
    load_tab = pltpu.make_async_copy(tab_ref, tab, insem.at[2])
    load_near.start()
    load_x.start()
    barrier = pltpu.get_barrier_semaphore()

    def z_peer(step):
        return (group, row * COLS_Z + lax.rem(column + step, COLS_Z))

    def y_peer(step):
        return (group, lax.rem(row + step, ROWS_Y) * COLS_Z + column)

    def group_peer(step):
        return (lax.rem(group + step, GROUPS), dev)

    stages = ((COLS_Z, z_peer), (ROWS_Y, y_peer), (GROUPS, group_peer))
    for count, peer in stages:
        for step in range(1, count):
            pl.semaphore_signal(barrier, inc=1, device_id=peer(step), device_id_type=MESH)
    load_near.wait()
    over = fill_tables(near_ref, row, column, tab_ref)
    load_tab.start()
    load_x.wait()
    tops[0, 0, 0:1] = jnp.max(local_signal(x_ref), axis=0, keepdims=True)
    tops[0, 0, 1:2] = over
    pack_faces(x_ref, own)
    load_tab.wait()
    pl.semaphore_wait(barrier, COLS_Z + ROWS_Y + GROUPS - 3)

    def small(stage, step):
        return pltpu.make_async_remote_copy(
            tops.at[stage, 0],
            tops.at[stage, step],
            tsend.at[stage, step],
            tgot.at[stage, step],
            device_id=stages[stage][1](step),
            device_id_type=MESH,
        )

    def send_top(stage):
        for step in range(1, stages[stage][0]):
            small(stage, step).start()

    def take_top(stage):
        count = stages[stage][0]
        for step in range(1, count):
            small(stage, step).wait()
        best = tops[stage, 0]
        for step in range(1, count):
            best = jnp.maximum(best, tops[stage, step])
        return best

    def z_copy(step):
        return pltpu.make_async_remote_copy(
            out_z.at[step],
            pool.at[pl.ds(OWN + (step - 1) * UNIT_Z, UNIT_Z)],
            zsend.at[step],
            zgot.at[step],
            device_id=z_peer(step),
            device_id_type=MESH,
        )

    def y_copy(step):
        return pltpu.make_async_remote_copy(
            out_y.at[step],
            got_ref.at[pl.ds((step - 1) * UNIT_Y, UNIT_Y)],
            ysend.at[step],
            ygot.at[step],
            device_id=y_peer(step),
            device_id_type=MESH,
        )

    send_top(0)
    for step in (4, 3, 5, 2, 6, 1, 7):
        entries = []
        for slot in range(CAP_Z):
            main = tab[0, step * CAP_Z + slot]
            entries.append((main, main + 2, None))
        move_records(own, entries, out_z.at[step], 0)
        z_copy(step).start()
    for tile in range(OWN):
        pool[tile] = own[tile]
    tops[1, 0] = take_top(0)
    send_top(1)
    tops[2, 0] = take_top(1)
    send_top(2)

    def records(first, count):
        return [tuple(tab[1 + part, first + slot] for part in range(3)) for slot in range(count)]

    for step in (1, 7, 2, 6, 3, 5, 4):
        z_copy(step).wait()
    for step in (2, 1, 3):
        move_records(pool, records((step - 1) * CAP_Y, CAP_Y), out_y.at[step], 0)
        y_copy(step).start()
    move_records(pool, records(3 * CAP_Y, CAP_HERE), got_ref, HERE)
    top_ref[...] = take_top(2)
    for step in (1, 3, 2):
        y_copy(step).wait()


def share(state, neighbours):
    vmem = pl.BlockSpec(memory_space=pltpu.VMEM)
    anywhere = pl.BlockSpec(memory_space=pl.ANY)
    return pl.pallas_call(
        share_kernel,
        out_shape=(
            jax.ShapeDtypeStruct((HERE + unit_tiles(CAP_HERE), 8, 128), jnp.float32),
            jax.ShapeDtypeStruct((2, 128), jnp.float32),
            jax.ShapeDtypeStruct((8, 128), jnp.int32),
        ),
        in_specs=[anywhere, anywhere],
        out_specs=(vmem, vmem, vmem),
        scratch_shapes=[
            pltpu.VMEM(state.shape, jnp.float32),
            pltpu.VMEM((2 * COLS_Z, 6), jnp.int32),
            pltpu.SMEM((8, 128), jnp.int32),
            pltpu.VMEM((OWN, 8, 128), jnp.float32),
            pltpu.VMEM((OWN + 7 * UNIT_Z, 8, 128), jnp.float32),
            pltpu.VMEM((COLS_Z, UNIT_Z, 8, 128), jnp.float32),
            pltpu.VMEM((ROWS_Y, UNIT_Y, 8, 128), jnp.float32),
            pltpu.VMEM((3, 8, 2, 128), jnp.float32),
            pltpu.SemaphoreType.DMA((3,)),
            pltpu.SemaphoreType.DMA((COLS_Z,)),
            pltpu.SemaphoreType.DMA((COLS_Z,)),
            pltpu.SemaphoreType.DMA((ROWS_Y,)),
            pltpu.SemaphoreType.DMA((ROWS_Y,)),
            pltpu.SemaphoreType.DMA((3, 8)),
            pltpu.SemaphoreType.DMA((3, 8)),
        ],
        compiler_params=pltpu.CompilerParams(
            collective_id=0, has_side_effects=True, vmem_limit_bytes=32 << 20
        ),
    )(state, neighbours)


def direct_kernel(base, table_ref, x_ref, got_ref, pool, out, ssem, rsem):
    group = lax.axis_index("group")
    dev = lax.axis_index("dev")
    barrier = pltpu.get_barrier_semaphore()

    def peer(step):
        return (group, lax.rem(dev + step, DEVS))

    def greet(step, carry):
        pl.semaphore_signal(barrier, inc=1, device_id=peer(step), device_id_type=MESH)
        return carry

    lax.fori_loop(1, DEVS, greet, 0)
    pack_faces(x_ref, pool)
    pl.semaphore_wait(barrier, DEVS - 1)

    def large(step):
        return pltpu.make_async_remote_copy(
            out.at[step],
            got_ref.at[step],
            ssem.at[step],
            rsem.at[step],
            device_id=peer(step),
            device_id_type=MESH,
        )

    def fill(step, target):
        entries = []
        for slot in (base, base + 1):
            main = table_ref[4 * step + slot] * RECORD
            entries.append((main, main + 2, None))
        move_records(pool, entries, target.at[step], 0)

    def send(step, carry):
        fill(step, out)
        large(step).start()
        return carry

    lax.fori_loop(1, DEVS, send, 0)
    fill(0, got_ref)

    def finish(step, carry):
        large(step).wait()
        return carry

    lax.fori_loop(1, DEVS, finish, 0)


def direct(table, state, base):
    vmem = pl.BlockSpec(memory_space=pltpu.VMEM)
    return pl.pallas_call(
        functools.partial(direct_kernel, base),
        out_shape=jax.ShapeDtypeStruct((DEVS, UNIT, 8, 128), jnp.float32),
        in_specs=[pl.BlockSpec(memory_space=pltpu.SMEM), vmem],
        out_specs=vmem,
        scratch_shapes=[
            pltpu.VMEM((OWN, 8, 128), jnp.float32),
            pltpu.VMEM((DEVS, UNIT, 8, 128), jnp.float32),
            pltpu.SemaphoreType.DMA((DEVS,)),
            pltpu.SemaphoreType.DMA((DEVS,)),
        ],
        compiler_params=pltpu.CompilerParams(
            collective_id=3 + base // 2, has_side_effects=True, vmem_limit_bytes=32 << 20
        ),
    )(table, state)


def rolled(arrays, amount, axis):
    return [pltpu.roll(a, amount % a.shape[axis], axis) for a in arrays]


def difference(states, normal, axis, unit):
    lefts, rights = [], []
    for field in states:
        (before,) = rolled([field], unit, axis)
        jump = field - before
        (after,) = rolled([jump], -unit, axis)
        half = 0.5 * minmod(jump, after)
        lefts.append(field + half)
        rights.append(field - half)
    fluxes = hll(rolled(lefts, unit, axis), rights, normal)
    return [high - low for high, low in zip(rolled(fluxes, -unit, axis), fluxes)]


def step_kernel(where_ref, owner_ref, x_ref, got_ref, top_ref, out_ref, turned_ref, total_ref, fresh, moved, ssem, rsem):
    group = lax.axis_index("group")
    dev = lax.axis_index("dev")
    parity = dev % 2
    partner = (group, dev + 1 - 2 * parity)
    border = 1 - parity
    barrier = pltpu.get_barrier_semaphore()
    pl.semaphore_signal(barrier, inc=1, device_id=partner, device_id_type=MESH)
    ratio = COURANT / jnp.max(top_ref[0:1, :], axis=(0, 1), keepdims=True)
    matrix = swap_matrix(PLANE, lambda layer: layer)
    lane = lanes(EDGE)
    half = lanes(8) < 64
    row8 = lax.broadcasted_iota(jnp.int32, (8, PLANE), 0)

    def fetch(box, face):
        spot = box * 6 + face
        main = where_ref[4, spot]
        main = jnp.concatenate([got_ref[main], got_ref[main + 1]], axis=0)
        extra = got_ref[where_ref[5, spot]]
        side = jnp.full((8, 128), where_ref[6, spot], jnp.int32)
        extra = jnp.where(side == 0, extra, pltpu.roll(extra, 64, 1))
        return main, extra, where_ref[7, spot]

    def lane_ghosts(main, extra, target):
        out = []
        for field in range(4):
            out.append(pltpu.roll(main, (target - 32 * field) % 128, 1))
        first = pltpu.roll(extra, target % 128, 1)
        second = pltpu.roll(extra, (target - 32) % 128, 1)
        out.append(jnp.concatenate([first, second], axis=0))
        return out

    def row_ghosts(main, extra):
        out = []
        last = jnp.where(half[0:4], extra[0:4], pltpu.roll(extra, 64, 1)[4:8])
        for field in range(FIELDS):
            rows = main[4 * field : 4 * field + 4] if field < 4 else last
            out.append(
                [
                    jnp.concatenate([rows[2 * layer : 2 * layer + 1], rows[2 * layer + 1 : 2 * layer + 2]], axis=1)
                    for layer in range(2)
                ]
            )
        return out

    copy = pltpu.make_async_remote_copy(
        fresh.at[border], moved, ssem, rsem, device_id=partner, device_id_type=MESH
    )

    def one_box(index, carry):
        box = lax.rem(border + index, 2)
        cells = [x_ref[box, field] for field in range(FIELDS)]
        turned_ref[...] = exact_permute(jnp.concatenate(cells, axis=0), matrix)
        low_main, low_extra, low_there = fetch(box, 0)
        high_main, high_extra, high_there = fetch(box, 1)
        low = row_ghosts(low_main, low_extra)
        high = row_ghosts(high_main, high_extra)
        low_there = jnp.full((1, PLANE), low_there, jnp.int32) > 0
        high_there = jnp.full((1, PLANE), high_there, jnp.int32) > 0
        extended = []
        for field in range(FIELDS):
            edge_low = cells[field][0:1]
            edge_high = cells[field][EDGE - 1 : EDGE]
            l0 = jnp.where(low_there, low[field][0], edge_low)
            l1 = jnp.where(low_there, low[field][1], edge_low)
            h0 = jnp.where(high_there, high[field][0], edge_high)
            h1 = jnp.where(high_there, high[field][1], edge_high)
            tile = jnp.where(row8 == 0, h0, jnp.where(row8 == 7, l1, jnp.where(row8 == 6, l0, h1)))
            extended.append(jnp.concatenate([cells[field], tile], axis=0))
        for part in range(2):
            states = primitive([e[:, 128 * part : 128 * part + 128] for e in extended])
            parts = difference(states, 0, 0, 1)
            for field in range(FIELDS):
                total_ref[field, :, 128 * part : 128 * part + 128] = parts[field][0:EDGE]
        for axis in (2, 1):
            if axis == 1:
                source = cells
            else:
                source = [turned_ref[EDGE * f : EDGE * f + EDGE] for f in range(FIELDS)]
            low_main, low_extra, low_there = fetch(box, 2 * axis)
            high_main, high_extra, high_there = fetch(box, 2 * axis + 1)
            there = jnp.where(lane < 64, jnp.full((EDGE, 128), high_there, jnp.int32), low_there) > 0
            low = lane_ghosts(low_main, low_extra, 96)
            high = lane_ghosts(high_main, high_extra, 0)
            extended = []
            for field in range(FIELDS):
                left, right = source[field][:, 0:128], source[field][:, 128:256]
                edge_low = jnp.where(lane < 112, pltpu.roll(left, 96, 1), pltpu.roll(left, 112, 1))
                edge_high = jnp.where(lane < 16, pltpu.roll(right, 16, 1), pltpu.roll(right, 32, 1))
                ghost = jnp.where(lane < 64, high[field], low[field])
                tile = jnp.where(there, ghost, jnp.where(lane < 64, edge_high, edge_low))
                extended.append(jnp.concatenate([left, right, tile], axis=1))
            pieces = []
            for part in range(2):
                states = primitive([e[8 * part : 8 * part + 8] for e in extended])
                pieces.append(difference(states, axis, 1, EDGE))
            if axis == 2:
                stacked = jnp.concatenate(
                    [pieces[part][f][:, 0:PLANE] for f in range(FIELDS) for part in range(2)], axis=0
                )
                turned_ref[...] = exact_permute(stacked, matrix)
            else:
                for field in range(FIELDS):
                    along = jnp.concatenate([pieces[part][field][:, 0:PLANE] for part in range(2)], axis=0)
                    total = (total_ref[field] + along) + turned_ref[EDGE * field : EDGE * field + EDGE]
                    fresh[box, field] = cells[field] - ratio * total

        @pl.when(index == 0)
        def _():
            pl.semaphore_wait(barrier, 1)
            copy.start()

        return carry

    lax.fori_loop(0, 2, one_box, 0)
    copy.wait()
    pair = (group * DEVS + dev) // 2
    split = jnp.zeros((EDGE, PLANE), jnp.int32)
    for box in range(4):
        split = split + jnp.where(jnp.full((EDGE, PLANE), owner_ref[4 * pair + box], jnp.int32) == 2 * pair, 1, 0)
    lower = jnp.full((EDGE, PLANE), parity, jnp.int32) == 0
    for field in range(FIELDS):
        zero, one, other = fresh[0, field], fresh[1, field], moved[field]
        none = jnp.zeros_like(zero)
        early = jnp.where(split == 1, other, jnp.where(split == 2, zero, one))
        out_ref[0, field] = jnp.where(lower, zero, early)
        low = jnp.where(split >= 2, one, none)
        high = jnp.where(split == 1, zero, jnp.where(split == 2, one, none))
        out_ref[1, field] = jnp.where(lower, low, high)
        low = jnp.where(split == 3, other, none)
        high = jnp.where(split == 1, one, none)
        out_ref[2, field] = jnp.where(lower, low, high)


def advance(where, new_owner, state, got, top, number):
    vmem = pl.BlockSpec(memory_space=pltpu.VMEM)
    box = state.shape[1:]
    return pl.pallas_call(
        step_kernel,
        out_shape=jax.ShapeDtypeStruct((3,) + box, state.dtype),
        in_specs=[pl.BlockSpec(memory_space=pltpu.SMEM)] * 2 + [vmem] * 3,
        out_specs=vmem,
        scratch_shapes=[
            pltpu.VMEM((FIELDS * EDGE, PLANE), jnp.float32),
            pltpu.VMEM((FIELDS, EDGE, PLANE), jnp.float32),
            pltpu.VMEM((2,) + box, jnp.float32),
            pltpu.VMEM(box, jnp.float32),
            pltpu.SemaphoreType.DMA,
            pltpu.SemaphoreType.DMA,
        ],
        compiler_params=pltpu.CompilerParams(
            collective_id=number, has_side_effects=True, vmem_limit_bytes=32 << 20
        ),
    )(where, new_owner, state, got, top)


def count(test, axis):
    return jnp.sum(test.astype(jnp.int32), axis=axis)


def direct_tables(near, dev):
    face = jnp.arange(FACES, dtype=jnp.int32)
    there = near >= 0
    other = jnp.where(there, (near // 2) % DEVS, -1)
    same = (other[:, None] == other[None, :]) & there[:, None] & there[None, :]
    rank = count(same & (face[None, :] < face[:, None]), 1)
    far_face = (near % 2) * 6 + ((face % 6) ^ 1)
    far_rank = count(same & (far_face[None, :] < far_face[:, None]), 1)
    place = jnp.where(there, ((other - dev + DEVS) % DEVS) * 4 + rank, -1)
    spot = jnp.arange(4 * DEVS, dtype=jnp.int32)
    hit = spot[:, None] == place[None, :]
    table = FACES + jnp.sum(jnp.where(hit, face[None, :] - FACES, 0), axis=1)
    begin = (((dev - other + DEVS) % DEVS) * 2 + far_rank // 2) * UNIT
    where = jnp.stack([begin + 2 * (far_rank % 2), begin + 4, far_rank % 2, jnp.ones_like(near)])
    return table, jnp.pad(jnp.where(there, where, 0), ((4, 0), (0, 128 - FACES)))


def body(state, new_owner, neighbours):
    group = lax.axis_index("group")
    dev = lax.axis_index("dev")
    got, top, where = share(state, neighbours)

    def fits(state):
        return advance(where, new_owner, state, got, top, 1)

    def crowded(state):
        near = lax.dynamic_slice_in_dim(neighbours, 2 * (group * DEVS + dev), 2, 0).reshape(FACES)
        table, where = direct_tables(near, dev)
        both = jnp.concatenate([direct(table, state, 0), direct(table, state, 2)], axis=1)
        return advance(where, new_owner, state, both.reshape(-1, 8, 128), top, 2)

    return lax.cond(top[1, 0] > 0.5, crowded, fits, state)


def solution(mesh):
    placed = (P(("group", "dev"), None, None, None), P(), P())
    return jax.shard_map(
        body,
        mesh=mesh,
        in_specs=placed,
        out_specs=P(("group", "dev"), None, None, None),
        check_vma=False,
    )
```
